32 devices in a mesh: leaf: 2 (over core), seq: 16 (over z, y, x).
Axes of the slice: x: 2, y: 2, z: 4, core: 2. Of those that a mesh axis runs over, the one named last changes fastest.
Arguments:
- queries: bfloat16 [2, 4096, 4096], P('leaf', 'seq'), may hold values from -40 to 40
- branch_key_rows: bfloat16 [2, 4096, 512], P('leaf', 'seq'), may hold values from -6 to 6
- branch_value_rows: bfloat16 [2, 4096, 512], P('leaf', 'seq'), may hold values from -6 to 6
- grad_output: bfloat16 [2, 4096, 4096], P('leaf', 'seq'), may hold values from -6 to 6
- trunk_keys: bfloat16 [2, 256, 512], P('leaf', 'seq'), may hold values from -6 to 6
- trunk_token_values: bfloat16 [2, 256, 512], P('leaf', 'seq'), may hold values from -6 to 6
- lengths: int32 [2, 64], P(None, 'seq'), may hold values from 0 to 64, as said below
- parents: int32 [2, 64], P(None, 'seq'), may hold values from 1 to 255
Outputs:
- grad_queries: float32 [2, 4096, 4096], P('leaf', 'seq')
- grad_branch_keys: float32 [2, 4096, 512], P('leaf', 'seq')
- grad_branch_values: float32 [2, 4096, 512], P('leaf', 'seq')
- grad_trunk_keys: float32 [2, 256, 512], P('leaf', 'seq')
- grad_trunk_values: float32 [2, 256, 512], P('leaf', 'seq')
The draws below stay inside these ranges and needn't reach their ends.
Inputs may be any that keep to these rules, and one draw needn't show every extreme that they name: `lengths`: 0 means that the slot holds no branch.
All inputs are finite; a program needn't handle non-finite values.
Results may differ from the reference program's by a relative error of at most 0.0052.
Values may be sent and summed in bfloat16 or wider, within the bound.
A program may use at most 64 MiB of HBM per device.

```python
import math
import jax
import jax.numpy as jnp
from jax import lax

QUERY_HEADS = 32
KEY_VALUE_HEADS = 4
HEAD_SIZE = 128
TRUNK_TOKENS = 256
TILE_ROWS = 64
TILES_DEV = 4
ROLLOUT_TREES = 2
BRANCH_SLOTS = 64


def trunk_base(key):
    drawn_values = jnp.clip(jax.random.normal(jax.random.fold_in(key, 11), (ROLLOUT_TREES, TRUNK_TOKENS, KEY_VALUE_HEADS * HEAD_SIZE), jnp.float32), -6.0, 6.0)
    return drawn_values


def draw_trunk_keys(key, part):
    return trunk_base(key).astype(jnp.bfloat16)


def draw_queries(key, part):
    drawn_values = jnp.clip(jax.random.normal(jax.random.fold_in(key, 21), (ROLLOUT_TREES, BRANCH_SLOTS * TILE_ROWS, QUERY_HEADS * HEAD_SIZE), jnp.float32), -6.0, 6.0)
    return drawn_values.astype(jnp.bfloat16)


def draw_lengths(key, part):
    half_trees = ROLLOUT_TREES // 2
    tree_ids = jnp.arange(ROLLOUT_TREES)[:, None]
    heavy_side = jax.random.randint(jax.random.fold_in(key, 37), (half_trees,), 0, 2)
    side_of_tree = jnp.concatenate([heavy_side, 1 - heavy_side])[:, None]
    heavy_level = jax.random.randint(jax.random.fold_in(key, 31), (ROLLOUT_TREES, 1), 70, 101)
    light_level = jax.random.randint(jax.random.fold_in(key, 38), (ROLLOUT_TREES, 1), 10, 31)
    fill_level = jnp.where(side_of_tree == 1, heavy_level, light_level)
    roll_value = jax.random.randint(jax.random.fold_in(key, 32), (ROLLOUT_TREES, BRANCH_SLOTS), 0, 100)
    branch_size = jax.random.randint(jax.random.fold_in(key, 33), (ROLLOUT_TREES, BRANCH_SLOTS), 1, TILE_ROWS + 1)
    found = jnp.where(roll_value < fill_level, branch_size, 0)
    pair_index = jax.random.randint(jax.random.fold_in(key, 34), (), 0, half_trees)
    column = jax.random.randint(jax.random.fold_in(key, 35), (), 0, BRANCH_SLOTS // TILES_DEV)
    flip_side = jax.random.randint(jax.random.fold_in(key, 36), (), 0, 2)
    giver_tree = pair_index + flip_side * half_trees
    taker_tree = pair_index + (1 - flip_side) * half_trees
    branch_ids = jnp.arange(BRANCH_SLOTS)[None, :]
    in_column = branch_ids // TILES_DEV == column
    found = jnp.where((tree_ids == giver_tree) & in_column, jnp.maximum(found, 1), found)
    found = jnp.where((tree_ids == taker_tree) & in_column, 0, found)
    found = jnp.where((tree_ids == giver_tree) & (branch_ids == column * TILES_DEV), TILE_ROWS, found)
    return found.astype(jnp.int32)


def place_ends(result, rng, least, largest):
    longest = result.shape.index(max(result.shape))
    spots = []
    for shift in (0, 1):
        where = [jax.random.randint(jax.random.fold_in(rng, axis), (), 0, length) for axis, length in enumerate(result.shape)]
        where[longest] = (where[longest] + shift) % result.shape[longest]
        spots.append(tuple(where))
    return result.at[spots[0]].set(least).at[spots[1]].set(largest)


def shard_levels(key, shape, shards, least, high):
    def one(position, parts):
        heights = jax.random.uniform(jax.random.fold_in(jax.random.fold_in(key, 6), position), (parts,), jnp.float32, least / len(shards), high / len(shards))
        return jnp.repeat(jnp.exp(heights), shape[position] // parts).reshape((-1,) + (1,) * (len(shape) - position - 1))

    loudness = one(*shards[0])
    for cut in shards[1:]:
        loudness = loudness * one(*cut)
    return loudness


def normal_values(own_key, extent, width, bound, shards=(), held_as=jnp.bfloat16):
    drawn = jax.random.normal(own_key, extent, jnp.float32) * width
    if len(shards) > 0:
        drawn = shard_levels(own_key, extent, shards, -0.22, 0.18) * drawn
    return jnp.clip(drawn, min=-bound, max=bound).astype(held_as)


def setup_inputs(seed: int = 0) -> dict:
    streams_of = jax.random.split(jax.random.key(seed), 9)
    queries = draw_queries(jax.random.fold_in(streams_of[8], 71), 0)
    branch_key_rows = normal_values(streams_of[1], (ROLLOUT_TREES, BRANCH_SLOTS * TILE_ROWS, KEY_VALUE_HEADS * HEAD_SIZE), 1.0, 6.0, ((0, 2), (1, 16)))
    branch_value_rows = normal_values(streams_of[2], (ROLLOUT_TREES, BRANCH_SLOTS * TILE_ROWS, KEY_VALUE_HEADS * HEAD_SIZE), 1.0, 6.0, ((0, 2), (1, 16)))
    grad_output = normal_values(streams_of[3], (ROLLOUT_TREES, BRANCH_SLOTS * TILE_ROWS, QUERY_HEADS * HEAD_SIZE), 1.0, 6.0, ((0, 2), (1, 16)))
    trunk_keys = draw_trunk_keys(jax.random.fold_in(streams_of[8], 71), 0)
    trunk_token_values = normal_values(streams_of[5], (ROLLOUT_TREES, TRUNK_TOKENS, KEY_VALUE_HEADS * HEAD_SIZE), 1.0, 6.0, ((0, 2), (1, 16)))
    lengths = draw_lengths(jax.random.fold_in(streams_of[8], 71), 0)
    parents = place_ends(jax.random.randint(streams_of[7], (ROLLOUT_TREES, BRANCH_SLOTS), 1, TRUNK_TOKENS), jax.random.fold_in(streams_of[7], 1), 1, TRUNK_TOKENS - 1).astype(jnp.int32)
    return {"queries": queries, "branch_key_rows": branch_key_rows, "branch_value_rows": branch_value_rows, "grad_output": grad_output, "trunk_keys": trunk_keys, "trunk_token_values": trunk_token_values, "lengths": lengths, "parents": parents}


masked_score = -1e+30

def tile_grads(tile_items):
    query_rows, grad_rows, key_rows, value_rows, trunk_keys_all, trunk_vals_all, length, parent = tile_items
    row_count = query_rows.shape[0]
    trunk_len = trunk_keys_all.shape[0]
    width_span = QUERY_HEADS // KEY_VALUE_HEADS * HEAD_SIZE
    score_scale = 1.0 / math.sqrt(HEAD_SIZE)
    all_keys = jnp.concatenate([trunk_keys_all, key_rows], axis=0).astype(jnp.float32)
    all_values = jnp.concatenate([trunk_vals_all, value_rows], axis=0).astype(jnp.float32)
    row_ids = lax.broadcasted_iota(jnp.int32, (row_count, trunk_len + row_count), 0)
    col_ids = lax.broadcasted_iota(jnp.int32, (row_count, trunk_len + row_count), 1)
    allowed = jnp.where(col_ids < trunk_len, col_ids <= parent, col_ids - trunk_len <= row_ids)
    live_rows = (lax.broadcasted_iota(jnp.int32, (row_count, 1), 0) < length).astype(jnp.float32)
    query_parts, key_parts, value_parts = ([], [], [])
    for index_of_head in range(KEY_VALUE_HEADS):
        query_head = query_rows[:, index_of_head * width_span:(index_of_head + 1) * width_span].astype(jnp.float32).reshape(row_count, width_span // HEAD_SIZE, HEAD_SIZE)
        grad_head = grad_rows[:, index_of_head * width_span:(index_of_head + 1) * width_span].astype(jnp.float32).reshape(row_count, width_span // HEAD_SIZE, HEAD_SIZE)
        key_head = all_keys[:, index_of_head * HEAD_SIZE:(index_of_head + 1) * HEAD_SIZE]
        value_head = all_values[:, index_of_head * HEAD_SIZE:(index_of_head + 1) * HEAD_SIZE]
        scores = jnp.einsum('igd,jd->gij', query_head, key_head, precision=lax.Precision.HIGHEST) * score_scale
        scores = jnp.where(allowed[None], scores, masked_score)
        row_peak = lax.optimization_barrier(jnp.max(scores, axis=-1, keepdims=True))
        exponent = jnp.where(allowed[None], jnp.exp(scores - row_peak), 0.0)
        weights = exponent / lax.optimization_barrier(jnp.sum(exponent, axis=-1, keepdims=True)) * live_rows[None]
        weights_low = weights.astype(jnp.bfloat16).astype(jnp.float32)
        grad_weights = jnp.einsum('igd,jd->gij', grad_head, value_head, precision=lax.Precision.HIGHEST)
        row_delta = lax.optimization_barrier(jnp.sum(weights * grad_weights, axis=-1, keepdims=True))
        dscore = (weights * (grad_weights - row_delta) * score_scale).astype(jnp.bfloat16).astype(jnp.float32)
        query_parts.append(jnp.einsum('gij,jd->igd', dscore, key_head, precision=lax.Precision.HIGHEST).reshape(row_count, width_span))
        key_parts.append(jnp.einsum('gij,igd->jd', dscore, query_head, precision=lax.Precision.HIGHEST))
        value_parts.append(jnp.einsum('gij,igd->jd', weights_low, grad_head, precision=lax.Precision.HIGHEST))
    return (jnp.concatenate(query_parts, axis=1), jnp.concatenate(key_parts, axis=1), jnp.concatenate(value_parts, axis=1))

def skipped(tile_items):
    row_count = tile_items[0].shape[0]
    total = tile_items[4].shape[0] + row_count
    return (jnp.zeros((row_count, tile_items[0].shape[1]), jnp.float32), jnp.zeros((total, tile_items[2].shape[1]), jnp.float32), jnp.zeros((total, tile_items[2].shape[1]), jnp.float32))

def one_tree(tree_items):
    query_full, gradient_full, key_full, value_full, trunk_keys_all, trunk_vals_all, length_per_tree, parent_per_tree = tree_items

    def one_tile(partial_sums, slot_entries):
        query_rows, grad_rows, key_rows, value_rows, length, parent = slot_entries
        results = lax.cond(length > 0, tile_grads, skipped, (query_rows, grad_rows, key_rows, value_rows, trunk_keys_all, trunk_vals_all, length, parent))
        new_sums = (partial_sums[0] + results[1][:TRUNK_TOKENS], partial_sums[1] + results[2][:TRUNK_TOKENS])
        return (new_sums, (results[0], results[1][TRUNK_TOKENS:], results[2][TRUNK_TOKENS:]))
    initial_sums = (jnp.zeros((TRUNK_TOKENS, KEY_VALUE_HEADS * HEAD_SIZE), jnp.float32), jnp.zeros((TRUNK_TOKENS, KEY_VALUE_HEADS * HEAD_SIZE), jnp.float32))
    slot_entries = (query_full.reshape(BRANCH_SLOTS, TILE_ROWS, QUERY_HEADS * HEAD_SIZE), gradient_full.reshape(BRANCH_SLOTS, TILE_ROWS, QUERY_HEADS * HEAD_SIZE), key_full.reshape(BRANCH_SLOTS, TILE_ROWS, KEY_VALUE_HEADS * HEAD_SIZE), value_full.reshape(BRANCH_SLOTS, TILE_ROWS, KEY_VALUE_HEADS * HEAD_SIZE), length_per_tree, parent_per_tree)
    trunk_partial_sums, tile_outputs = lax.scan(one_tile, initial_sums, slot_entries)
    return (tile_outputs[0].reshape(BRANCH_SLOTS * TILE_ROWS, QUERY_HEADS * HEAD_SIZE), tile_outputs[1].reshape(BRANCH_SLOTS * TILE_ROWS, KEY_VALUE_HEADS * HEAD_SIZE), tile_outputs[2].reshape(BRANCH_SLOTS * TILE_ROWS, KEY_VALUE_HEADS * HEAD_SIZE), trunk_partial_sums[0], trunk_partial_sums[1])

def reference(queries, branch_key_rows, branch_value_rows, grad_output, trunk_keys, trunk_token_values, lengths, parents):
    results = lax.map(one_tree, (queries, grad_output, branch_key_rows, branch_value_rows, trunk_keys, trunk_token_values, lengths, parents))
    return (results[0], results[1], results[2], results[3], results[4])
```

```python
import functools
import math

import jax
import jax.numpy as jnp
from jax import lax
from jax.experimental import pallas as pl
from jax.experimental.pallas import tpu as pltpu
from jax.sharding import PartitionSpec as P

HEAD_SIZE = 128
MASKED = -1e30
DIRECT = 1


def tile_width(rows, group):
    return rows * math.gcd(group, max(1, 256 // rows))


def drain(ref, sem):
    pltpu.make_async_copy(ref, ref, sem).wait()


def remote(axis, peer, src, dst, send_sem, recv_sem):
    return pltpu.make_async_remote_copy(
        src_ref=src,
        dst_ref=dst,
        send_sem=send_sem,
        recv_sem=recv_sem,
        device_id={axis: peer},
        device_id_type=pl.DeviceIdType.MESH,
    )


def fused_kernel(
    axis,
    outer,
    inner,
    len_ref,
    par_ref,
    q_hbm,
    g_hbm,
    bk_hbm,
    bv_hbm,
    tk_hbm,
    tv_hbm,
    dq_ref,
    dbk_ref,
    dbv_ref,
    dt_ref,
    q_buf,
    g_buf,
    bk_buf,
    bv_buf,
    score_buf,
    trunk_buf,
    stage,
    landed,
    trunk_bias,
    branch_bias,
    load_sem,
    own_sem,
    gather_send,
    gather_recv,
    scatter_send,
    scatter_recv,
):
    count = outer * inner
    me = lax.axis_index(axis)
    line, place = lax.div(me, inner), lax.rem(me, inner)
    heads, rows_dev, group_width = q_buf.shape
    own = tk_hbm.shape[1]
    trunk = trunk_buf.shape[2]
    slots = len_ref.shape[1]
    rows = rows_dev // slots
    group = group_width // HEAD_SIZE
    width = branch_bias.shape[1]
    tiles = width // rows
    bf16, f32 = jnp.bfloat16, jnp.float32
    tree = lax.axis_index("leaf")
    others = (count - 1) * own

    def block(peer):
        return pl.ds(pl.multiple_of(peer * own, own), own)

    def line_at(offset):
        return lax.rem(line + outer + offset, outer)

    def peer_at(step):
        return lax.rem(me + step, count)

    def loads(head):
        copies = []
        for i, (src, dst) in enumerate(
            ((q_hbm, q_buf), (bk_hbm, bk_buf), (g_hbm, g_buf), (bv_hbm, bv_buf))
        ):
            wide = dst.shape[2]
            span = slice(head * wide, (head + 1) * wide)
            copies.append(
                pltpu.make_async_copy(src.at[0, :, span], dst.at[head], load_sem.at[i, head])
            )
        return copies

    def own_copies(head):
        span = slice(head * HEAD_SIZE, (head + 1) * HEAD_SIZE)
        return [
            pltpu.make_async_copy(
                src.at[0, :, span], trunk_buf.at[head, i, block(me)], own_sem.at[i, head]
            )
            for i, src in ((0, tk_hbm), (1, tv_hbm))
        ]

    def gather_all(head, step):
        spot = trunk_buf.at[head, :, block(me)]
        return remote(
            axis, peer_at(step), spot, spot, gather_send.at[head], gather_recv.at[head, 0]
        )

    def gather_line(head, step):
        spot = trunk_buf.at[head, :, block(me)]
        return remote(
            axis,
            line_at(step) * inner + place,
            spot,
            spot,
            gather_send.at[head],
            gather_recv.at[head, step],
        )

    def gather_plane(head, back, step):
        spot = trunk_buf.at[head, :, block(line_at(-back) * inner + place)]
        return remote(
            axis,
            line * inner + lax.rem(place + step, inner),
            spot,
            spot,
            gather_send.at[head],
            gather_recv.at[head, 0],
        )

    def pass_on(head):
        for back in range(outer):
            if back:
                gather_line(head, back).wait_recv()
            for step in range(1, inner):
                gather_plane(head, back, step).start()

    def arrive(head):
        if head < DIRECT:
            drain(trunk_buf.at[head, :, pl.ds(0, others)], gather_recv.at[head, 0])
        else:
            drain(
                trunk_buf.at[head, :, pl.ds(0, outer * (inner - 1) * own)], gather_recv.at[head, 0]
            )

    def scatter(head, step):
        target = peer_at(step)
        return remote(
            axis,
            target,
            stage.at[head, :, block(target)],
            landed.at[head, step],
            scatter_send.at[head],
            scatter_recv.at[head],
        )

    barrier = pltpu.get_barrier_semaphore()
    for step in range(1, count):
        pl.semaphore_signal(
            barrier,
            inc=1,
            device_id={axis: peer_at(step)},
            device_id_type=pl.DeviceIdType.MESH,
        )
    for head in range(heads):
        for copy in own_copies(head):
            copy.start()
    for head in range(heads):
        for copy in loads(head):
            copy.start()
    token_ids = lax.broadcasted_iota(jnp.int32, (trunk, HEAD_SIZE), 0)
    for slot in range(slots):
        trunk_bias[slot] = jnp.where(token_ids <= par_ref[tree, slot], 0.0, MASKED)
    key_ids = lax.broadcasted_iota(jnp.int32, (rows, width), 0)
    row_ids = lax.rem(lax.broadcasted_iota(jnp.int32, (rows, width), 1), rows)
    branch_bias[...] = jnp.where(key_ids <= row_ids, 0.0, MASKED)
    pl.semaphore_wait(barrier, count - 1)
    for head in range(heads):
        for copy in own_copies(head):
            copy.wait()
        if head < DIRECT:
            for step in range(1, count):
                gather_all(head, step).start()
        else:
            for step in range(1, outer):
                gather_line(head, step).start()

    scale = 1.0 / math.sqrt(HEAD_SIZE)
    to_log2 = scale * math.log2(math.e)
    contract_last = (((1,), (1,)), ((), ()))
    contract_first = (((0,), (0,)), ((), ()))
    row_of_lane = lax.rem(lax.broadcasted_iota(jnp.int32, (1, width), 1), rows)

    def one_head(head, relays):
        arrive(head)
        for copy in loads(head):
            copy.wait()
        parts = [(slot, first) for slot in range(slots) for first in range(0, group, tiles)]
        trunk_k, trunk_v = trunk_buf[head, 0], trunk_buf[head, 1]
        sums = {}

        def stacked(ref, slot, first):
            span = slice(slot * rows, (slot + 1) * rows)
            return jnp.concatenate(
                [
                    ref[head, span, g * HEAD_SIZE : (g + 1) * HEAD_SIZE]
                    for g in range(first, first + tiles)
                ],
                axis=0,
            )

        def products(slot, first):
            span = slice(slot * rows, (slot + 1) * rows)
            query, cotangent = stacked(q_buf, slot, first), stacked(g_buf, slot, first)
            keys = jnp.concatenate([trunk_k, bk_buf[head, span, :]], axis=0)
            values = jnp.concatenate([trunk_v, bv_buf[head, span, :]], axis=0)
            scores = lax.dot_general(keys, query, contract_last, preferred_element_type=f32)
            grad_weights = lax.dot_general(
                values, cotangent, contract_last, preferred_element_type=f32
            )
            return query, cotangent, scores, grad_weights

        def softmax(slot, scores, grad_weights):
            bias = jnp.concatenate([trunk_bias[slot]] * (width // HEAD_SIZE), axis=1)
            scores = jnp.concatenate(
                [scores[:trunk] + bias, scores[trunk:] + branch_bias[...]], axis=0
            )
            peak = jnp.max(scores, axis=0, keepdims=True)
            exponent = jnp.exp2(scores * to_log2 - peak * to_log2)
            live = jnp.where(row_of_lane < len_ref[tree, slot], 1.0, 0.0)
            weights = exponent * (live / jnp.sum(exponent, axis=0, keepdims=True))
            delta = jnp.sum(weights * grad_weights, axis=0, keepdims=True)
            dscore = weights * ((grad_weights - delta) * scale)
            return weights.astype(bf16), dscore.astype(bf16)

        def add(name, value):
            sums[name] = sums[name] + value if name in sums else value

        def gradients(slot, first, query, cotangent, weights, dscore):
            score_buf[head, slot, :, first * rows : first * rows + width] = dscore
            dk = jnp.dot(dscore, query, preferred_element_type=f32)
            dv = jnp.dot(weights, cotangent, preferred_element_type=f32)
            add("trunk_k", dk[:trunk])
            add("trunk_v", dv[:trunk])
            add(("k", slot), dk[trunk:])
            add(("v", slot), dv[trunk:])
            if first + tiles == group:
                span = slice(slot * rows, (slot + 1) * rows)
                dbk_ref[head, span, :] = sums[("k", slot)]
                dbv_ref[head, span, :] = sums[("v", slot)]

        ahead, behind = products(*parts[0]), None
        for i, part in enumerate(parts):
            query, cotangent, scores, grad_weights = ahead
            if i + 1 < len(parts):
                ahead = products(*parts[i + 1])
            weights, dscore = softmax(part[0], scores, grad_weights)
            if behind is not None:
                gradients(*behind)
            behind = (*part, query, cotangent, weights, dscore)
            if i in relays:
                pass_on(relays[i])
        gradients(*behind)
        stage[head, 0] = sums["trunk_k"].astype(bf16)
        stage[head, 1] = sums["trunk_v"].astype(bf16)
        for step in range(1, count):
            scatter(head, step).start()

    def query_grads(head, carry):
        for slot in range(slots):
            span = slice(slot * rows, (slot + 1) * rows)
            keys = jnp.concatenate([trunk_buf[head, 0], bk_buf[head, span, :]], axis=0)
            dq = lax.dot_general(
                score_buf[head, slot], keys, contract_first, preferred_element_type=f32
            )
            for g in range(group):
                dq_ref[head, span, g * HEAD_SIZE : (g + 1) * HEAD_SIZE] = dq[
                    g * rows : (g + 1) * rows
                ]
        return carry

    steps = slots * (group // tiles)
    plan = {head: {} for head in range(heads)}
    early = []
    for head in range(DIRECT, heads):
        at = (head - DIRECT) * steps // 2
        if at == 0:
            early.append(head)
        else:
            plan[at // steps][at % steps] = head
    for head in early:
        pass_on(head)
    for head in range(heads):
        one_head(head, plan[head])
    lax.fori_loop(0, heads, query_grads, 0)

    def finish(head, carry):
        drain(landed.at[head, pl.ds(1, count - 1)], scatter_recv.at[head])
        total = stage[head, :, block(me), :].astype(f32)
        for step in range(1, count):
            total += landed[head, step].astype(f32)
        dt_ref[head] = total
        drain(trunk_buf.at[head, :, pl.ds(0, others)], gather_send.at[head])
        drain(stage.at[head, :, pl.ds(0, others)], scatter_send.at[head])
        return carry

    lax.fori_loop(0, heads, finish, 0)


def write_kernel(dq_ref, dbk_ref, dbv_ref, dt_ref, dq_out, dbk_out, dbv_out, dtk_out, dtv_out, sem):
    heads = dq_ref.shape[0]
    copies = []
    for head in range(heads):
        for i, (src, dst) in enumerate(
            (
                (dq_ref.at[head], dq_out),
                (dbk_ref.at[head], dbk_out),
                (dbv_ref.at[head], dbv_out),
                (dt_ref.at[head, 0], dtk_out),
                (dt_ref.at[head, 1], dtv_out),
            )
        ):
            wide = src.shape[1]
            target = dst.at[0, :, head * wide : (head + 1) * wide]
            copies.append(pltpu.make_async_copy(src, target, sem.at[i, head]))
    for copy in copies:
        copy.start()
    for copy in copies:
        copy.wait()


def per_device(count, q, bk, bv, g, tk, tv, lengths, parents):
    rows, columns = q.shape[1:]
    kv_columns = bk.shape[2]
    heads = kv_columns // HEAD_SIZE
    own, trunk = tk.shape[1], tk.shape[1] * count
    slots = lengths.shape[1]
    per_slot = columns // kv_columns * (rows // slots)
    inner = 1 << (count.bit_length() - 1) // 2
    while count % inner:
        inner //= 2
    outer = count // inner
    f32, bf16 = jnp.float32, jnp.bfloat16
    smem = pl.BlockSpec(memory_space=pltpu.SMEM)
    vmem = pl.BlockSpec(memory_space=pltpu.VMEM)
    hbm = pl.BlockSpec(memory_space=pltpu.HBM)
    held = (
        (heads, rows, columns // heads),
        (heads, rows, HEAD_SIZE),
        (heads, rows, HEAD_SIZE),
        (heads, 2, own, HEAD_SIZE),
    )
    results = pl.pallas_call(
        functools.partial(fused_kernel, "seq", outer, inner),
        out_shape=[pltpu.VMEM(shape, f32) for shape in held],
        in_specs=[smem, smem] + [hbm] * 6,
        out_specs=[vmem] * len(held),
        scratch_shapes=[
            pltpu.VMEM((heads, rows, columns // heads), bf16),
            pltpu.VMEM((heads, rows, columns // heads), bf16),
            pltpu.VMEM((heads, rows, HEAD_SIZE), bf16),
            pltpu.VMEM((heads, rows, HEAD_SIZE), bf16),
            pltpu.VMEM((heads, slots, trunk + rows // slots, per_slot), bf16),
            pltpu.VMEM((heads, 2, trunk, HEAD_SIZE), bf16),
            pltpu.VMEM((heads, 2, trunk, HEAD_SIZE), bf16),
            pltpu.VMEM((heads, count, 2, own, HEAD_SIZE), bf16),
            pltpu.VMEM((slots, trunk, HEAD_SIZE), f32),
            pltpu.VMEM((rows // slots, tile_width(rows // slots, columns // kv_columns)), f32),
            pltpu.SemaphoreType.DMA((4, heads)),
            pltpu.SemaphoreType.DMA((2, heads)),
            pltpu.SemaphoreType.DMA((heads,)),
            pltpu.SemaphoreType.DMA((heads, outer)),
            pltpu.SemaphoreType.DMA((heads,)),
            pltpu.SemaphoreType.DMA((heads,)),
        ],
        compiler_params=pltpu.CompilerParams(
            collective_id=0, has_side_effects=True, vmem_limit_bytes=40 << 20
        ),
        name="fused",
    )(
        *[
            pltpu.with_memory_space_constraint(x, pltpu.HBM)
            for x in (lengths, parents, q, g, bk, bv, tk, tv)
        ]
    )
    results = [pltpu.with_memory_space_constraint(x, pltpu.VMEM) for x in results]
    shapes = (q.shape, bk.shape, bv.shape, tk.shape, tv.shape)
    return pl.pallas_call(
        write_kernel,
        out_shape=[jax.ShapeDtypeStruct(shape, f32) for shape in shapes],
        in_specs=[pl.BlockSpec(memory_space=pl.ANY)] * len(held),
        out_specs=[hbm] * len(shapes),
        scratch_shapes=[pltpu.SemaphoreType.DMA((len(shapes), heads))],
        compiler_params=pltpu.CompilerParams(vmem_limit_bytes=4 << 20),
        name="write_out",
    )(*results)


def solution(mesh):
    tall = P("leaf", "seq", None)
    return jax.shard_map(
        functools.partial(per_device, mesh.shape["seq"]),
        mesh=mesh,
        in_specs=(tall,) * 6 + (P(None, "seq"),) * 2,
        out_specs=(tall,) * 5,
        check_vma=False,
    )
```

```python
import functools
import math

import jax
import jax.numpy as jnp
from jax import lax
from jax.experimental import pallas as pl
from jax.experimental.pallas import tpu as pltpu
from jax.sharding import PartitionSpec as P

HEAD_SIZE = 128
MASKED = -1e30


def tile_width(rows, group):
    return rows * math.gcd(group, max(1, 256 // rows))


def gather_groups(heads):
    alone = min(2, heads)
    return [(head, 1) for head in range(alone)] + [(alone, heads - alone)] * (heads > alone)


def drain(ref, sem):
    pltpu.make_async_copy(ref, ref, sem).wait()


def remote(axis, peer, src, dst, send_sem, recv_sem):
    return pltpu.make_async_remote_copy(
        src_ref=src,
        dst_ref=dst,
        send_sem=send_sem,
        recv_sem=recv_sem,
        device_id={axis: peer},
        device_id_type=pl.DeviceIdType.MESH,
    )


def fused_kernel(
    axis,
    outer,
    inner,
    len_hbm,
    par_hbm,
    q_hbm,
    g_hbm,
    bk_hbm,
    bv_hbm,
    tk_hbm,
    tv_hbm,
    dq_ref,
    dbk_ref,
    dbv_ref,
    dt_ref,
    q_buf,
    g_buf,
    bk_buf,
    bv_buf,
    score_buf,
    trunk_buf,
    stage,
    landed,
    branch_buf,
    trunk_bias,
    branch_bias,
    len_ref,
    par_ref,
    load_sem,
    own_sem,
    table_sem,
    gather_send,
    gather_recv,
    scatter_send,
    scatter_recv,
):
    count = outer * inner
    me = lax.axis_index(axis)
    line, place = lax.div(me, inner), lax.rem(me, inner)
    heads, rows_dev, group_width = q_buf.shape
    own = tk_hbm.shape[1]
    trunk = trunk_buf.shape[2]
    slots = len_ref.shape[1]
    rows = rows_dev // slots
    group = group_width // HEAD_SIZE
    width = branch_bias.shape[1]
    tiles = width // rows
    bf16, f32 = jnp.bfloat16, jnp.float32
    tree = lax.axis_index("leaf")
    others = (count - 1) * own

    def block(peer):
        return pl.ds(pl.multiple_of(peer * own, own), own)

    def line_at(offset):
        return lax.rem(line + outer + offset, outer)

    def peer_at(step):
        return lax.rem(me + step, count)

    def loads(head):
        copies = []
        for i, (src, dst) in enumerate(
            ((q_hbm, q_buf), (bk_hbm, bk_buf), (g_hbm, g_buf), (bv_hbm, bv_buf))
        ):
            wide = dst.shape[2]
            span = slice(head * wide, (head + 1) * wide)
            copies.append(
                pltpu.make_async_copy(src.at[0, :, span], dst.at[head], load_sem.at[i, head])
            )
        return copies

    def own_copies(head):
        span = slice(head * HEAD_SIZE, (head + 1) * HEAD_SIZE)
        return [
            pltpu.make_async_copy(
                src.at[0, :, span], trunk_buf.at[head, i, block(me)], own_sem.at[i, head]
            )
            for i, src in ((0, tk_hbm), (1, tv_hbm))
        ]

    groups = [pl.ds(first, size) for first, size in gather_groups(heads)]

    def gather_line(i, step):
        spot = trunk_buf.at[groups[i], :, block(me)]
        return remote(
            axis,
            line_at(step) * inner + place,
            spot,
            spot,
            gather_send.at[i],
            gather_recv.at[i, step],
        )

    def gather_plane(i, back, step):
        spot = trunk_buf.at[groups[i], :, block(line_at(-back) * inner + place)]
        return remote(
            axis,
            line * inner + lax.rem(place + step, inner),
            spot,
            spot,
            gather_send.at[i],
            gather_recv.at[i, 0],
        )

    def pass_on(i):
        for back in range(outer):
            if back:
                gather_line(i, back).wait_recv()
            for step in range(1, inner):
                gather_plane(i, back, step).start()

    def arrive(i):
        drain(
            trunk_buf.at[groups[i], :, pl.ds(0, outer * (inner - 1) * own)], gather_recv.at[i, 0]
        )

    def scatter(head, step):
        target = peer_at(step)
        return remote(
            axis,
            target,
            stage.at[head, :, block(target)],
            landed.at[head, step],
            scatter_send.at[head],
            scatter_recv.at[head],
        )

    barrier = pltpu.get_barrier_semaphore()
    for step in range(1, count):
        pl.semaphore_signal(
            barrier,
            inc=1,
            device_id={axis: peer_at(step)},
            device_id_type=pl.DeviceIdType.MESH,
        )
    for head in range(heads):
        for copy in own_copies(head):
            copy.start()
    tables = [
        pltpu.make_async_copy(src, dst, table_sem.at[i])
        for i, (src, dst) in enumerate(((len_hbm, len_ref), (par_hbm, par_ref)))
    ]
    for copy in tables:
        copy.start()
    for head in range(heads):
        for copy in loads(head):
            copy.start()
    pl.semaphore_wait(barrier, count - 1)
    for head in range(heads):
        for copy in own_copies(head):
            copy.wait()
    for i in range(len(groups)):
        for step in range(1, outer):
            gather_line(i, step).start()

    for copy in tables:
        copy.wait()
    token_ids = lax.broadcasted_iota(jnp.int32, (trunk, HEAD_SIZE), 0)
    for slot in range(slots):
        trunk_bias[slot] = jnp.where(token_ids <= par_ref[tree, slot], 0.0, MASKED)
    key_ids = lax.broadcasted_iota(jnp.int32, (rows, width), 0)
    row_ids = lax.rem(lax.broadcasted_iota(jnp.int32, (rows, width), 1), rows)
    branch_bias[...] = jnp.where(key_ids <= row_ids, 0.0, MASKED)
    scale = 1.0 / math.sqrt(HEAD_SIZE)
    to_log2 = scale * math.log2(math.e)
    contract_last = (((1,), (1,)), ((), ()))
    contract_first = (((0,), (0,)), ((), ()))
    row_of_lane = lax.rem(lax.broadcasted_iota(jnp.int32, (1, width), 1), rows)

    def stacked(ref, head, slot, first, size):
        span = slice(slot * rows, (slot + 1) * rows)
        return jnp.concatenate(
            [
                ref[head, span, g * HEAD_SIZE : (g + 1) * HEAD_SIZE]
                for g in range(first, first + size)
            ],
            axis=0,
        )

    def branch_products(head):
        for copy in loads(head):
            copy.wait()
        for slot in range(slots):
            span = slice(slot * rows, (slot + 1) * rows)
            for first in range(0, group, tiles):
                lanes = slice(first * rows, first * rows + width)
                scores = lax.dot_general(
                    bk_buf[head, span, :],
                    stacked(q_buf, head, slot, first, tiles),
                    contract_last,
                    preferred_element_type=f32,
                )
                branch_buf[head, slot, 0, :, lanes] = scores + branch_bias[...]
                branch_buf[head, slot, 1, :, lanes] = lax.dot_general(
                    bv_buf[head, span, :],
                    stacked(g_buf, head, slot, first, tiles),
                    contract_last,
                    preferred_element_type=f32,
                )

    def one_head(head):
        for i, (first, _) in enumerate(gather_groups(heads)):
            if first == head:
                arrive(i)
        parts = [(slot, first) for slot in range(slots) for first in range(0, group, tiles)]
        trunk_k, trunk_v = trunk_buf[head, 0], trunk_buf[head, 1]
        sums = {}

        def products(slot, first):
            query = stacked(q_buf, head, slot, first, tiles)
            cotangent = stacked(g_buf, head, slot, first, tiles)
            scores = lax.dot_general(trunk_k, query, contract_last, preferred_element_type=f32)
            grad_weights = lax.dot_general(
                trunk_v, cotangent, contract_last, preferred_element_type=f32
            )
            return query, cotangent, scores, grad_weights

        def softmax(slot, first, scores, grad_weights):
            lanes = slice(first * rows, first * rows + width)
            bias = jnp.concatenate([trunk_bias[slot]] * (width // HEAD_SIZE), axis=1)
            scores = jnp.concatenate([scores + bias, branch_buf[head, slot, 0, :, lanes]], axis=0)
            grad_weights = jnp.concatenate(
                [grad_weights, branch_buf[head, slot, 1, :, lanes]], axis=0
            )
            peak = jnp.max(scores, axis=0, keepdims=True)
            exponent = jnp.exp2(scores * to_log2 - peak * to_log2)
            live = jnp.where(row_of_lane < len_ref[tree, slot], 1.0, 0.0)
            weights = exponent * (live / jnp.sum(exponent, axis=0, keepdims=True))
            delta = jnp.sum(weights * grad_weights, axis=0, keepdims=True)
            dscore = weights * ((grad_weights - delta) * scale)
            return weights.astype(bf16), dscore.astype(bf16)

        def add(name, value):
            sums[name] = sums[name] + value if name in sums else value

        def gradients(slot, first, query, cotangent, weights, dscore):
            score_buf[head, slot, :, first * rows : first * rows + width] = dscore
            dk = jnp.dot(dscore, query, preferred_element_type=f32)
            dv = jnp.dot(weights, cotangent, preferred_element_type=f32)
            add("trunk_k", dk[:trunk])
            add("trunk_v", dv[:trunk])
            add(("k", slot), dk[trunk:])
            add(("v", slot), dv[trunk:])
            if first + tiles == group:
                span = slice(slot * rows, (slot + 1) * rows)
                dbk_ref[head, span, :] = sums[("k", slot)]
                dbv_ref[head, span, :] = sums[("v", slot)]

        ahead, behind = products(*parts[0]), None
        for i, part in enumerate(parts):
            query, cotangent, scores, grad_weights = ahead
            if i + 1 < len(parts):
                ahead = products(*parts[i + 1])
            weights, dscore = softmax(*part, scores, grad_weights)
            if behind is not None:
                gradients(*behind)
            behind = (*part, query, cotangent, weights, dscore)
        gradients(*behind)
        stage[head, 0] = sums["trunk_k"].astype(bf16)
        stage[head, 1] = sums["trunk_v"].astype(bf16)
        for step in range(1, count):
            scatter(head, step).start()

    def query_grads(head, carry):
        for slot in range(slots):
            span = slice(slot * rows, (slot + 1) * rows)
            keys = jnp.concatenate([trunk_buf[head, 0], bk_buf[head, span, :]], axis=0)
            dq = lax.dot_general(
                score_buf[head, slot], keys, contract_first, preferred_element_type=f32
            )
            for g in range(group):
                dq_ref[head, span, g * HEAD_SIZE : (g + 1) * HEAD_SIZE] = dq[
                    g * rows : (g + 1) * rows
                ]
        return carry

    for i, (first, size) in enumerate(gather_groups(heads)):
        for head in range(first, first + size):
            branch_products(head)
        pass_on(i)
    for head in range(heads):
        one_head(head)
    lax.fori_loop(0, heads, query_grads, 0)

    for head in range(heads):
        drain(landed.at[head, pl.ds(1, count - 1)], scatter_recv.at[head])
        total = stage[head, :, block(me), :].astype(f32)
        for step in range(1, count):
            total += landed[head, step].astype(f32)
        dt_ref[head] = total
    for i, spot in enumerate(groups):
        drain(trunk_buf.at[spot, :, pl.ds(0, others)], gather_send.at[i])
    for head in range(heads):
        drain(stage.at[head, :, pl.ds(0, others)], scatter_send.at[head])


def write_kernel(dq_ref, dbk_ref, dbv_ref, dt_ref, dq_out, dbk_out, dbv_out, dtk_out, dtv_out, sem):
    heads = dq_ref.shape[0]
    copies = []
    for head in range(heads):
        for i, (src, dst) in enumerate(
            (
                (dq_ref.at[head], dq_out),
                (dbk_ref.at[head], dbk_out),
                (dbv_ref.at[head], dbv_out),
                (dt_ref.at[head, 0], dtk_out),
                (dt_ref.at[head, 1], dtv_out),
            )
        ):
            wide = src.shape[1]
            target = dst.at[0, :, head * wide : (head + 1) * wide]
            copies.append(pltpu.make_async_copy(src, target, sem.at[i, head]))
    for copy in copies:
        copy.start()
    for copy in copies:
        copy.wait()


def per_device(count, q, bk, bv, g, tk, tv, lengths, parents):
    rows, columns = q.shape[1:]
    kv_columns = bk.shape[2]
    heads = kv_columns // HEAD_SIZE
    own, trunk = tk.shape[1], tk.shape[1] * count
    slots = lengths.shape[1]
    per_slot = columns // kv_columns * (rows // slots)
    inner = 1 << (count.bit_length() - 1) // 2
    while count % inner:
        inner //= 2
    outer = count // inner
    f32, bf16 = jnp.float32, jnp.bfloat16
    vmem = pl.BlockSpec(memory_space=pltpu.VMEM)
    hbm = pl.BlockSpec(memory_space=pltpu.HBM)
    held = (
        (heads, rows, columns // heads),
        (heads, rows, HEAD_SIZE),
        (heads, rows, HEAD_SIZE),
        (heads, 2, own, HEAD_SIZE),
    )
    results = pl.pallas_call(
        functools.partial(fused_kernel, "seq", outer, inner),
        out_shape=[pltpu.VMEM(shape, f32) for shape in held],
        in_specs=[hbm] * 8,
        out_specs=[vmem] * len(held),
        scratch_shapes=[
            pltpu.VMEM((heads, rows, columns // heads), bf16),
            pltpu.VMEM((heads, rows, columns // heads), bf16),
            pltpu.VMEM((heads, rows, HEAD_SIZE), bf16),
            pltpu.VMEM((heads, rows, HEAD_SIZE), bf16),
            pltpu.VMEM((heads, slots, trunk + rows // slots, per_slot), bf16),
            pltpu.VMEM((heads, 2, trunk, HEAD_SIZE), bf16),
            pltpu.VMEM((heads, 2, trunk, HEAD_SIZE), bf16),
            pltpu.VMEM((heads, count, 2, own, HEAD_SIZE), bf16),
            pltpu.VMEM((heads, slots, 2, rows // slots, per_slot), f32),
            pltpu.VMEM((slots, trunk, HEAD_SIZE), f32),
            pltpu.VMEM((rows // slots, tile_width(rows // slots, columns // kv_columns)), f32),
            pltpu.SMEM(lengths.shape, jnp.int32),
            pltpu.SMEM(parents.shape, jnp.int32),
            pltpu.SemaphoreType.DMA((4, heads)),
            pltpu.SemaphoreType.DMA((2, heads)),
            pltpu.SemaphoreType.DMA((2,)),
            pltpu.SemaphoreType.DMA((heads,)),
            pltpu.SemaphoreType.DMA((heads, outer)),
            pltpu.SemaphoreType.DMA((heads,)),
            pltpu.SemaphoreType.DMA((heads,)),
        ],
        compiler_params=pltpu.CompilerParams(
            collective_id=0, has_side_effects=True, vmem_limit_bytes=40 << 20
        ),
        name="fused",
    )(
        *[
            pltpu.with_memory_space_constraint(x, pltpu.HBM)
            for x in (lengths, parents, q, g, bk, bv, tk, tv)
        ]
    )
    results = [pltpu.with_memory_space_constraint(x, pltpu.VMEM) for x in results]
    shapes = (q.shape, bk.shape, bv.shape, tk.shape, tv.shape)
    return pl.pallas_call(
        write_kernel,
        out_shape=[jax.ShapeDtypeStruct(shape, f32) for shape in shapes],
        in_specs=[pl.BlockSpec(memory_space=pl.ANY)] * len(held),
        out_specs=[hbm] * len(shapes),
        scratch_shapes=[pltpu.SemaphoreType.DMA((len(shapes), heads))],
        compiler_params=pltpu.CompilerParams(vmem_limit_bytes=4 << 20),
        name="write_out",
    )(*results)


def solution(mesh):
    tall = P("leaf", "seq", None)
    return jax.shard_map(
        functools.partial(per_device, mesh.shape["seq"]),
        mesh=mesh,
        in_specs=(tall,) * 6 + (P(None, "seq"),) * 2,
        out_specs=(tall,) * 5,
        check_vma=False,
    )
```

```python
import functools
import math

import jax
import jax.numpy as jnp
from jax import lax
from jax.experimental import pallas as pl
from jax.experimental.pallas import tpu as pltpu
from jax.sharding import PartitionSpec as P

HEAD_SIZE = 128
MASKED = -1e30


def tile_width(rows, group):
    return rows * math.gcd(group, max(1, 256 // rows))


def gather_groups(heads):
    alone = min(2, heads)
    return [(head, 1) for head in range(alone)] + [(alone, heads - alone)] * (heads > alone)


def drain(ref, sem):
    pltpu.make_async_copy(ref, ref, sem).wait()


def remote(axis, peer, src, dst, send_sem, recv_sem):
    return pltpu.make_async_remote_copy(
        src_ref=src,
        dst_ref=dst,
        send_sem=send_sem,
        recv_sem=recv_sem,
        device_id={axis: peer},
        device_id_type=pl.DeviceIdType.MESH,
    )


def fused_kernel(
    axis,
    outer,
    inner,
    len_hbm,
    par_hbm,
    q_hbm,
    g_hbm,
    bk_hbm,
    bv_hbm,
    tk_hbm,
    tv_hbm,
    dq_ref,
    dbk_ref,
    dbv_ref,
    dt_ref,
    q_buf,
    g_buf,
    bk_buf,
    bv_buf,
    score_buf,
    trunk_buf,
    stage,
    landed,
    branch_buf,
    trunk_bias,
    branch_bias,
    len_ref,
    par_ref,
    load_sem,
    own_sem,
    table_sem,
    gather_send,
    gather_recv,
    scatter_send,
    scatter_recv,
):
    count = outer * inner
    me = lax.axis_index(axis)
    line, place = lax.div(me, inner), lax.rem(me, inner)
    heads, rows_dev, group_width = q_buf.shape
    own = tk_hbm.shape[1]
    trunk = trunk_buf.shape[2]
    slots = len_ref.shape[1]
    rows = rows_dev // slots
    group = group_width // HEAD_SIZE
    width = branch_bias.shape[1]
    tiles = width // rows
    bf16, f32 = jnp.bfloat16, jnp.float32
    tree = lax.axis_index("leaf")
    others = (count - 1) * own

    def block(peer):
        return pl.ds(pl.multiple_of(peer * own, own), own)

    def line_at(offset):
        return lax.rem(line + outer + offset, outer)

    def peer_at(step):
        return lax.rem(me + step, count)

    def loads(head):
        copies = []
        for i, (src, dst) in enumerate(
            ((q_hbm, q_buf), (bk_hbm, bk_buf), (g_hbm, g_buf), (bv_hbm, bv_buf))
        ):
            wide = dst.shape[2]
            span = slice(head * wide, (head + 1) * wide)
            copies.append(
                pltpu.make_async_copy(src.at[0, :, span], dst.at[head], load_sem.at[i, head])
            )
        return copies

    def own_copies(head):
        span = slice(head * HEAD_SIZE, (head + 1) * HEAD_SIZE)
        return [
            pltpu.make_async_copy(
                src.at[0, :, span], trunk_buf.at[head, i, block(me)], own_sem.at[i, head]
            )
            for i, src in ((0, tk_hbm), (1, tv_hbm))
        ]

    groups = [pl.ds(first, size) for first, size in gather_groups(heads)]

    def gather_line(i, step):
        spot = trunk_buf.at[groups[i], :, block(me)]
        return remote(
            axis,
            line_at(step) * inner + place,
            spot,
            spot,
            gather_send.at[i],
            gather_recv.at[i, step],
        )

    def gather_plane(i, back, step):
        spot = trunk_buf.at[groups[i], :, block(line_at(-back) * inner + place)]
        return remote(
            axis,
            line * inner + lax.rem(place + step, inner),
            spot,
            spot,
            gather_send.at[i],
            gather_recv.at[i, 0],
        )

    def pass_on(i):
        for back in range(outer):
            if back:
                gather_line(i, back).wait_recv()
            for step in range(1, inner):
                gather_plane(i, back, step).start()

    def arrive(i):
        drain(
            trunk_buf.at[groups[i], :, pl.ds(0, outer * (inner - 1) * own)], gather_recv.at[i, 0]
        )

    def scatter(head, step):
        target = peer_at(step)
        return remote(
            axis,
            target,
            stage.at[head, :, block(target)],
            landed.at[head, step],
            scatter_send.at[head],
            scatter_recv.at[head],
        )

    barrier = pltpu.get_barrier_semaphore()
    for step in range(1, count):
        pl.semaphore_signal(
            barrier,
            inc=1,
            device_id={axis: peer_at(step)},
            device_id_type=pl.DeviceIdType.MESH,
        )
    for head in range(heads):
        for copy in own_copies(head):
            copy.start()
    tables = [
        pltpu.make_async_copy(src, dst, table_sem.at[i])
        for i, (src, dst) in enumerate(((len_hbm, len_ref), (par_hbm, par_ref)))
    ]
    for copy in tables:
        copy.start()
    for head in range(heads):
        for copy in loads(head):
            copy.start()
    pl.semaphore_wait(barrier, count - 1)
    for i, (first, size) in enumerate(gather_groups(heads)):
        for head in range(first, first + size):
            for copy in own_copies(head):
                copy.wait()
        for step in range(1, outer):
            gather_line(i, step).start()

    for copy in tables:
        copy.wait()
    token_ids = lax.broadcasted_iota(jnp.int32, (trunk, HEAD_SIZE), 0)
    for slot in range(slots):
        trunk_bias[slot] = jnp.where(token_ids <= par_ref[tree, slot], 0.0, MASKED)
    key_ids = lax.broadcasted_iota(jnp.int32, (rows, width), 0)
    row_ids = lax.rem(lax.broadcasted_iota(jnp.int32, (rows, width), 1), rows)
    branch_bias[...] = jnp.where(key_ids <= row_ids, 0.0, MASKED)
    scale = 1.0 / math.sqrt(HEAD_SIZE)
    to_log2 = scale * math.log2(math.e)
    contract_last = (((1,), (1,)), ((), ()))
    contract_first = (((0,), (0,)), ((), ()))
    row_of_lane = lax.rem(lax.broadcasted_iota(jnp.int32, (1, width), 1), rows)

    def stacked(ref, head, slot, first, size):
        span = slice(slot * rows, (slot + 1) * rows)
        return jnp.concatenate(
            [
                ref[head, span, g * HEAD_SIZE : (g + 1) * HEAD_SIZE]
                for g in range(first, first + size)
            ],
            axis=0,
        )

    def branch_products(head):
        for copy in loads(head):
            copy.wait()
        for slot in range(slots):
            span = slice(slot * rows, (slot + 1) * rows)
            for first in range(0, group, tiles):
                lanes = slice(first * rows, first * rows + width)
                scores = lax.dot_general(
                    bk_buf[head, span, :],
                    stacked(q_buf, head, slot, first, tiles),
                    contract_last,
                    preferred_element_type=f32,
                )
                branch_buf[head, slot, 0, :, lanes] = scores + branch_bias[...]
                branch_buf[head, slot, 1, :, lanes] = lax.dot_general(
                    bv_buf[head, span, :],
                    stacked(g_buf, head, slot, first, tiles),
                    contract_last,
                    preferred_element_type=f32,
                )

    def one_head(head):
        for i, (first, _) in enumerate(gather_groups(heads)):
            if first == head:
                arrive(i)
        parts = [(slot, first) for slot in range(slots) for first in range(0, group, tiles)]
        trunk_k, trunk_v = trunk_buf[head, 0], trunk_buf[head, 1]
        sums = {}

        def products(slot, first):
            query = stacked(q_buf, head, slot, first, tiles)
            cotangent = stacked(g_buf, head, slot, first, tiles)
            scores = lax.dot_general(trunk_k, query, contract_last, preferred_element_type=f32)
            grad_weights = lax.dot_general(
                trunk_v, cotangent, contract_last, preferred_element_type=f32
            )
            return query, cotangent, scores, grad_weights

        def softmax(slot, first, scores, grad_weights):
            lanes = slice(first * rows, first * rows + width)
            bias = jnp.concatenate([trunk_bias[slot]] * (width // HEAD_SIZE), axis=1)
            scores = jnp.concatenate([scores + bias, branch_buf[head, slot, 0, :, lanes]], axis=0)
            grad_weights = jnp.concatenate(
                [grad_weights, branch_buf[head, slot, 1, :, lanes]], axis=0
            )
            peak = jnp.max(scores, axis=0, keepdims=True)
            exponent = jnp.exp2(scores * to_log2 - peak * to_log2)
            live = jnp.where(row_of_lane < len_ref[tree, slot], 1.0, 0.0)
            weights = exponent * (live / jnp.sum(exponent, axis=0, keepdims=True))
            delta = jnp.sum(weights * grad_weights, axis=0, keepdims=True)
            dscore = weights * ((grad_weights - delta) * scale)
            return weights.astype(bf16), dscore.astype(bf16)

        def add(name, value):
            sums[name] = sums[name] + value if name in sums else value

        def gradients(slot, first, query, cotangent, weights, dscore):
            score_buf[head, slot, :, first * rows : first * rows + width] = dscore
            dk = jnp.dot(dscore, query, preferred_element_type=f32)
            dv = jnp.dot(weights, cotangent, preferred_element_type=f32)
            add("trunk_k", dk[:trunk])
            add("trunk_v", dv[:trunk])
            add(("k", slot), dk[trunk:])
            add(("v", slot), dv[trunk:])
            if first + tiles == group:
                span = slice(slot * rows, (slot + 1) * rows)
                dbk_ref[head, span, :] = sums[("k", slot)]
                dbv_ref[head, span, :] = sums[("v", slot)]

        ahead, behind = products(*parts[0]), None
        for i, part in enumerate(parts):
            query, cotangent, scores, grad_weights = ahead
            if i + 1 < len(parts):
                ahead = products(*parts[i + 1])
            weights, dscore = softmax(*part, scores, grad_weights)
            if behind is not None:
                gradients(*behind)
            behind = (*part, query, cotangent, weights, dscore)
        gradients(*behind)
        stage[head, 0] = sums["trunk_k"].astype(bf16)
        stage[head, 1] = sums["trunk_v"].astype(bf16)
        for step in range(1, count):
            scatter(head, step).start()

    def query_grads(head, carry):
        for slot in range(slots):
            span = slice(slot * rows, (slot + 1) * rows)
            keys = jnp.concatenate([trunk_buf[head, 0], bk_buf[head, span, :]], axis=0)
            dq = lax.dot_general(
                score_buf[head, slot], keys, contract_first, preferred_element_type=f32
            )
            for g in range(group):
                dq_ref[head, span, g * HEAD_SIZE : (g + 1) * HEAD_SIZE] = dq[
                    g * rows : (g + 1) * rows
                ]
        return carry

    for i, (first, size) in enumerate(gather_groups(heads)):
        for head in range(first, first + size):
            branch_products(head)
        pass_on(i)
    for head in range(heads):
        one_head(head)
    lax.fori_loop(0, heads, query_grads, 0)

    for head in range(heads):
        drain(landed.at[head, pl.ds(1, count - 1)], scatter_recv.at[head])
        total = stage[head, :, block(me), :].astype(f32)
        for step in range(1, count):
            total += landed[head, step].astype(f32)
        dt_ref[head] = total
    for i, spot in enumerate(groups):
        drain(trunk_buf.at[spot, :, pl.ds(0, others)], gather_send.at[i])
    for head in range(heads):
        drain(stage.at[head, :, pl.ds(0, others)], scatter_send.at[head])


def write_kernel(dq_ref, dbk_ref, dbv_ref, dt_ref, dq_out, dbk_out, dbv_out, dtk_out, dtv_out, sem):
    heads = dq_ref.shape[0]
    copies = []
    for head in range(heads):
        for i, (src, dst) in enumerate(
            (
                (dq_ref.at[head], dq_out),
                (dbk_ref.at[head], dbk_out),
                (dbv_ref.at[head], dbv_out),
                (dt_ref.at[head, 0], dtk_out),
                (dt_ref.at[head, 1], dtv_out),
            )
        ):
            wide = src.shape[1]
            target = dst.at[0, :, head * wide : (head + 1) * wide]
            copies.append(pltpu.make_async_copy(src, target, sem.at[i, head]))
    for copy in copies:
        copy.start()
    for copy in copies:
        copy.wait()


def per_device(count, q, bk, bv, g, tk, tv, lengths, parents):
    rows, columns = q.shape[1:]
    kv_columns = bk.shape[2]
    heads = kv_columns // HEAD_SIZE
    own, trunk = tk.shape[1], tk.shape[1] * count
    slots = lengths.shape[1]
    per_slot = columns // kv_columns * (rows // slots)
    inner = 1 << (count.bit_length() - 1) // 2
    while count % inner:
        inner //= 2
    outer = count // inner
    f32, bf16 = jnp.float32, jnp.bfloat16
    vmem = pl.BlockSpec(memory_space=pltpu.VMEM)
    hbm = pl.BlockSpec(memory_space=pltpu.HBM)
    held = (
        (heads, rows, columns // heads),
        (heads, rows, HEAD_SIZE),
        (heads, rows, HEAD_SIZE),
        (heads, 2, own, HEAD_SIZE),
    )
    results = pl.pallas_call(
        functools.partial(fused_kernel, "seq", outer, inner),
        out_shape=[pltpu.VMEM(shape, f32) for shape in held],
        in_specs=[hbm] * 8,
        out_specs=[vmem] * len(held),
        scratch_shapes=[
            pltpu.VMEM((heads, rows, columns // heads), bf16),
            pltpu.VMEM((heads, rows, columns // heads), bf16),
            pltpu.VMEM((heads, rows, HEAD_SIZE), bf16),
            pltpu.VMEM((heads, rows, HEAD_SIZE), bf16),
            pltpu.VMEM((heads, slots, trunk + rows // slots, per_slot), bf16),
            pltpu.VMEM((heads, 2, trunk, HEAD_SIZE), bf16),
            pltpu.VMEM((heads, 2, trunk, HEAD_SIZE), bf16),
            pltpu.VMEM((heads, count, 2, own, HEAD_SIZE), bf16),
            pltpu.VMEM((heads, slots, 2, rows // slots, per_slot), f32),
            pltpu.VMEM((slots, trunk, HEAD_SIZE), f32),
            pltpu.VMEM((rows // slots, tile_width(rows // slots, columns // kv_columns)), f32),
            pltpu.SMEM(lengths.shape, jnp.int32),
            pltpu.SMEM(parents.shape, jnp.int32),
            pltpu.SemaphoreType.DMA((4, heads)),
            pltpu.SemaphoreType.DMA((2, heads)),
            pltpu.SemaphoreType.DMA((2,)),
            pltpu.SemaphoreType.DMA((heads,)),
            pltpu.SemaphoreType.DMA((heads, outer)),
            pltpu.SemaphoreType.DMA((heads,)),
            pltpu.SemaphoreType.DMA((heads,)),
        ],
        compiler_params=pltpu.CompilerParams(
            collective_id=0, has_side_effects=True, vmem_limit_bytes=40 << 20
        ),
        name="fused",
    )(
        *[
            pltpu.with_memory_space_constraint(x, pltpu.HBM)
            for x in (lengths, parents, q, g, bk, bv, tk, tv)
        ]
    )
    results = [pltpu.with_memory_space_constraint(x, pltpu.VMEM) for x in results]
    shapes = (q.shape, bk.shape, bv.shape, tk.shape, tv.shape)
    return pl.pallas_call(
        write_kernel,
        out_shape=[jax.ShapeDtypeStruct(shape, f32) for shape in shapes],
        in_specs=[pl.BlockSpec(memory_space=pl.ANY)] * len(held),
        out_specs=[hbm] * len(shapes),
        scratch_shapes=[pltpu.SemaphoreType.DMA((len(shapes), heads))],
        compiler_params=pltpu.CompilerParams(vmem_limit_bytes=4 << 20),
        name="write_out",
    )(*results)


def solution(mesh):
    tall = P("leaf", "seq", None)
    return jax.shard_map(
        functools.partial(per_device, mesh.shape["seq"]),
        mesh=mesh,
        in_specs=(tall,) * 6 + (P(None, "seq"),) * 2,
        out_specs=(tall,) * 5,
        check_vma=False,
    )
```
